32 devices in a mesh: clips: 2 (over x), seq: 16 (over z, y, core).
Axes of the slice: x: 2, y: 2, z: 4, core: 2. Of those that a mesh axis runs over, the one named last changes fastest.
Arguments:
- query_rows: bfloat16 [5120, 2560], P(('clips', 'seq')), parts along dimension 0, may hold values from -150 to 150
- key_rows: bfloat16 [5120, 2560], P(('clips', 'seq')), parts along dimension 0, may hold values from -7 to 7
- value_rows: bfloat16 [5120, 2560], P(('clips', 'seq')), parts along dimension 0, may hold values from -6 to 6
- target_rows: bfloat16 [5120, 2560], P(('clips', 'seq')), parts along dimension 0, may hold values from -6 to 6
- window: int32 [80, 10], replicated, may hold values from -1 to 79, as said below
Outputs:
- query_grad: bfloat16 [5120, 2560], P(('clips', 'seq')), parts along dimension 0
- key_grad: bfloat16 [5120, 2560], P(('clips', 'seq')), parts along dimension 0
- value_grad: bfloat16 [5120, 2560], P(('clips', 'seq')), parts along dimension 0
The draws below stay inside these ranges and needn't reach their ends.
There are 2 independent parts, one for each index of `clips`. The reference program is written for one: setup_inputs(seed, part) draws one part's arguments, and reference() takes and returns one part's arrays. A program takes and returns all parts, laid end to end along the dimension named above; an argument that names none is the same for every part. Nothing has to cross between parts.
Inputs may be any that keep to these rules, and one draw needn't show every extreme that they name: `window`: entry 0 of row t is t. Entries 1 to 4 are distinct tiles below t and the others distinct tiles above t, each at most 5 tiles from t; an entry whose tile would fall outside the clip is -1.
All inputs are finite; a program needn't handle non-finite values.
Results may differ from the reference program's by a relative error of at most 0.029.
The reference program's roundings to bfloat16 on the way count: a program that leaves them out, or rounds other values in their place, can miss the bound.
Values may be sent and summed in bfloat16 or wider, within the bound.
A program may use at most 64 MiB of HBM per device.

```python
import jax
import jax.numpy as jnp
from jax import lax

HEADS = 20
HD = 128
BT = 32
WIN = 10
TILE_DEV = 5
TILES = 80
TOKENS = 2560


def paired_draw(key):
    first_key, second_key = jax.random.split(jax.random.fold_in(key, 7), 2)
    key_values = jnp.clip(jax.random.normal(second_key, (TOKENS, HEADS * HD), jnp.float32), -6.0, 6.0)
    query_values = jnp.clip(jax.random.normal(first_key, (TOKENS, HEADS * HD), jnp.float32), -6.0, 6.0)
    return (query_values, key_values)


def draw_query_rows(key, part):
    return paired_draw(key)[0].astype(jnp.bfloat16)


def draw_key_rows(key, part):
    return paired_draw(key)[1].astype(jnp.bfloat16)


def draw_window(key, part):
    below_key, above_key = jax.random.split(jax.random.fold_in(key, 11))
    below_count = (WIN - 1) // 2
    above_count = WIN - 1 - below_count
    tile_index = jnp.arange(TILES, dtype=jnp.int32)[:, None]
    reach = jnp.arange(1, TILE_DEV + 1, dtype=jnp.int32)
    below_bits = jax.random.randint(below_key, (TILES, TILE_DEV), 0, 1 << 22) * 128 + reach[None, :]
    above_bits = jax.random.randint(above_key, (TILES, TILE_DEV), 0, 1 << 22) * 128 + reach[None, :]
    below_pick = reach[jnp.argsort(below_bits, axis=1)[:, :below_count]]
    above_pick = reach[jnp.argsort(above_bits, axis=1)[:, :above_count]]
    nearby = jnp.concatenate([tile_index - below_pick, tile_index + above_pick], axis=1)
    nearby = jnp.where((nearby >= 0) & (nearby < TILES), nearby, -1)
    return jnp.concatenate([tile_index, nearby], axis=1).astype(jnp.int32)


def steps_of(own_key, shape, pieces, least, largest):
    factor_of = 1.0
    for dim, shards_of in pieces:
        heights = jax.random.uniform(jax.random.fold_in(jax.random.fold_in(own_key, 6), dim), (shards_of,), jnp.float32, least / len(pieces), largest / len(pieces))
        factor_of = factor_of * jnp.repeat(jnp.exp(heights), shape[dim] // shards_of).reshape((-1,) + (1,) * (len(shape) - 1 - dim))
    return factor_of


def gaussian(key, shape, scale, most, shards=(), kind=jnp.bfloat16):
    factor_of = steps_of(key, shape, shards, -0.22, 0.18) if shards else 1.0
    array = jax.random.normal(key, shape, jnp.float32) * scale * factor_of
    return jnp.minimum(jnp.maximum(array, -most), most).astype(kind)


def setup_inputs(seed: int = 0, part: int = 0) -> dict:
    keys = jax.random.split(jax.random.key(seed), 6)
    own_keys = jax.random.split(jax.random.fold_in(keys[5], part), 6)
    return {
        "query_rows": draw_query_rows(jax.random.fold_in(jax.random.fold_in(keys[5], part), 71), part),
        "key_rows": draw_key_rows(jax.random.fold_in(jax.random.fold_in(keys[5], part), 71), part),
        "value_rows": gaussian(own_keys[2], (TOKENS, HEADS * HD), 1.0, 6.0, ((0, 16),)),
        "target_rows": gaussian(own_keys[3], (TOKENS, HEADS * HD), 1.0, 6.0, ((0, 16),)),
        "window": draw_window(jax.random.fold_in(keys[5], 71), part),
    }


def near_keys(window_rows, key_tiles, value_tiles):
    usable = window_rows >= 0
    position = jnp.where(usable, window_rows, 0).astype(jnp.int32)
    tile_count = window_rows.shape[0]
    keys_near = key_tiles[position].reshape(tile_count, WIN * BT, HEADS, HD)
    values_near = value_tiles[position].reshape(tile_count, WIN * BT, HEADS, HD)
    spread = jnp.repeat(usable, BT, axis=1)[:, None, None, :]
    return position, spread, keys_near, values_near


def forward_backward(block_queries, block_target, window_rows, key_tiles, value_tiles):
    score_scale = HD ** -0.5
    tile_count = block_queries.shape[0]
    position, spread, keys_near, values_near = near_keys(window_rows, key_tiles, value_tiles)
    scores = jnp.einsum("nqhd,nkhd->nhqk", block_queries.astype(jnp.float32), keys_near.astype(jnp.float32)) * score_scale
    highest_score = jnp.max(jnp.where(spread, scores, -1e30), axis=-1, keepdims=True)
    denominator = jnp.sum(jnp.where(spread, jnp.exp(scores - highest_score), 0.0), axis=-1, keepdims=True)
    log_total = highest_score + jnp.log(denominator)
    weights = jnp.where(spread, jnp.exp(scores - log_total), 0.0)
    weights_low = weights.astype(jnp.bfloat16)
    output = jnp.einsum("nhqk,nkhd->nqhd", weights_low.astype(jnp.float32), values_near.astype(jnp.float32))
    out_grad = (output - block_target.astype(jnp.float32)).astype(jnp.bfloat16)
    row_dot = jnp.transpose(jnp.sum(out_grad.astype(jnp.float32) * output, axis=-1), (0, 2, 1))[..., None]
    prob_grad = jnp.einsum("nqhd,nkhd->nhqk", out_grad.astype(jnp.float32), values_near.astype(jnp.float32))
    score_grad = (weights * (prob_grad - row_dot) * score_scale).astype(jnp.bfloat16)
    query_grad = jnp.einsum("nhqk,nkhd->nqhd", score_grad.astype(jnp.float32), keys_near.astype(jnp.float32))
    near_key = jnp.einsum("nhqk,nqhd->nkhd", score_grad.astype(jnp.float32), block_queries.astype(jnp.float32))
    near_value = jnp.einsum("nhqk,nqhd->nkhd", weights_low.astype(jnp.float32), out_grad.astype(jnp.float32))
    near_key = near_key.reshape(tile_count, WIN, BT, HEADS, HD)
    near_value = near_value.reshape(tile_count, WIN, BT, HEADS, HD)
    zeroed = jnp.zeros((key_tiles.shape[0], BT, HEADS, HD), jnp.float32)
    return query_grad, zeroed.at[position].add(near_key), zeroed.at[position].add(near_value)


def round_outside(partial_grad, first_tile):
    tile_index = jnp.arange(TILES, dtype=jnp.int32)
    inside = ((tile_index >= first_tile) & (tile_index < first_tile + TILE_DEV))[:, None, None, None]
    rounded = lax.optimization_barrier(partial_grad.astype(jnp.bfloat16)).astype(jnp.float32)
    return jnp.where(inside, partial_grad, rounded)


def reference(query_rows, key_rows, value_rows, target_rows, window):
    query_all = query_rows.reshape(TILES, BT, HEADS, HD)
    target_all = target_rows.reshape(TILES, BT, HEADS, HD)
    key_tiles = key_rows.reshape(TILES, BT, HEADS, HD)
    value_tiles = value_rows.reshape(TILES, BT, HEADS, HD)

    def block_step(running, block_index):
        first_tile = (block_index * TILE_DEV).astype(jnp.int32)
        block_queries = lax.dynamic_slice_in_dim(query_all, first_tile, TILE_DEV, 0)
        block_target = lax.dynamic_slice_in_dim(target_all, first_tile, TILE_DEV, 0)
        window_rows = lax.dynamic_slice_in_dim(window, first_tile, TILE_DEV, 0)
        query_grad, key_grad, value_grad = forward_backward(block_queries, block_target, window_rows, key_tiles, value_tiles)
        key_grad = round_outside(key_grad, first_tile)
        value_grad = round_outside(value_grad, first_tile)
        return (running[0] + key_grad, running[1] + value_grad), query_grad

    zeroed = jnp.zeros((TILES, BT, HEADS, HD), jnp.float32)
    running, query_grad = lax.scan(block_step, (zeroed, zeroed), jnp.arange(TILES // TILE_DEV, dtype=jnp.int32))
    return (query_grad.reshape(TOKENS, HEADS * HD).astype(jnp.bfloat16),
            running[0].reshape(TOKENS, HEADS * HD).astype(jnp.bfloat16),
            running[1].reshape(TOKENS, HEADS * HD).astype(jnp.bfloat16))
```

```python
import functools

import jax
import jax.numpy as jnp
from jax import lax
from jax.experimental import pallas as pl
from jax.experimental.pallas import tpu as pltpu
from jax.sharding import PartitionSpec as P

HEADS = 20
HD = 128
BT = 32
GROUP = 2
LOG2E = 1.4426950408889634


def dot(a, b, dims):
    return lax.dot_general(a, b, (dims, ((), ())), preferred_element_type=jnp.float32)


def kernel(
    count,
    win_ref,
    q_hbm,
    k_hbm,
    v_hbm,
    t_hbm,
    dq_ref,
    dk_ref,
    dv_ref,
    q_buf,
    t_buf,
    kx,
    vx,
    bias,
    acc_k,
    acc_v,
    part_k,
    part_v,
    got_k,
    got_v,
    local_sem,
    kv_send,
    kv_recv,
    part_send,
    part_recv,
):
    rows = q_buf.shape[0]
    tiles = rows // BT
    width = GROUP * HD
    groups = q_buf.shape[1] // width
    scale = HD ** (-0.5)
    me = lax.axis_index("seq")
    has = (me > 0, me < count - 1)
    peer = (me - 1, me + 1)
    place = (slice(0, rows), slice(2 * rows, 3 * rows))

    def columns(c):
        return pl.ds(pl.multiple_of(c * width, width), width)

    locals_ = [
        pltpu.make_async_copy(q_hbm, q_buf, local_sem.at[0]),
        pltpu.make_async_copy(k_hbm, kx.at[rows : 2 * rows], local_sem.at[1]),
        pltpu.make_async_copy(v_hbm, vx.at[rows : 2 * rows], local_sem.at[2]),
        pltpu.make_async_copy(t_hbm, t_buf, local_sem.at[3]),
    ]

    def kv_copy(side, arr, c, who):
        return pltpu.make_async_remote_copy(
            src_ref=(k_hbm, v_hbm)[arr].at[:, columns(c)],
            dst_ref=(kx, vx)[arr].at[place[1 - side], columns(c)],
            send_sem=kv_send.at[side, arr, c],
            recv_sem=kv_recv.at[1 - side, arr, c],
            device_id={"seq": who},
            device_id_type=pl.DeviceIdType.MESH,
        )

    def part_copy(side, arr, c, who):
        return pltpu.make_async_remote_copy(
            src_ref=(part_k, part_v)[arr].at[side, :, columns(c)],
            dst_ref=(got_k, got_v)[arr].at[1 - side, :, columns(c)],
            send_sem=part_send.at[side, arr, c],
            recv_sem=part_recv.at[1 - side, arr, c],
            device_id={"seq": who},
            device_id_type=pl.DeviceIdType.MESH,
        )

    barrier = pltpu.get_barrier_semaphore()
    for side in range(2):

        @pl.when(has[side])
        def _():
            pl.semaphore_signal(
                barrier,
                inc=1,
                device_id={"seq": peer[side]},
                device_id_type=pl.DeviceIdType.MESH,
            )

    for copy in locals_:
        copy.start()
    pl.semaphore_wait(barrier, has[0].astype(jnp.int32) + has[1].astype(jnp.int32))

    def send_group(c, carry):
        for side in range(2):

            @pl.when(has[side])
            def _():
                for arr in range(2):
                    kv_copy(side, arr, c, peer[side]).start()

        return carry

    lax.fori_loop(0, groups, send_group, 0)

    for side in range(2):

        @pl.when(jnp.logical_not(has[side]))
        def _():
            for buf in (kx, vx):
                buf[place[side]] = jnp.zeros((rows, buf.shape[1]), buf.dtype)
            for buf in (got_k, got_v):
                buf[side] = jnp.zeros(buf.shape[1:], buf.dtype)

    first = me * tiles
    listed = lax.broadcasted_iota(jnp.int32, (1, 3 * rows), 1) // BT + (first - tiles)
    for i in range(tiles):
        row_bias = jnp.full((1, 3 * rows), -1e30, jnp.float32)
        for j in range(win_ref.shape[1]):
            entry = win_ref[first + i, j]
            row_bias = jnp.where((listed == entry) & (listed >= 0), 0.0, row_bias)
        bias[i * BT : (i + 1) * BT] = jnp.broadcast_to(row_bias, (BT, 3 * rows))

    for copy in locals_:
        copy.wait()

    def one_head(col):
        cols = pl.ds(pl.multiple_of(col, HD), HD)
        q = q_buf[:, cols]
        k = kx[:, cols]
        v = vx[:, cols]
        s = dot(q, k, ((1,), (1,))) + bias[...]
        top = jnp.max(s, axis=-1, keepdims=True)
        e = jnp.exp2((s - top) * (scale * LOG2E))
        w = e * (1.0 / jnp.sum(e, axis=-1, keepdims=True))
        w_low = w.astype(jnp.bfloat16)
        out = dot(w_low, v, ((1,), (0,)))
        og = (out - t_buf[:, cols].astype(jnp.float32)).astype(jnp.bfloat16)
        rd = jnp.sum(og.astype(jnp.float32) * out, axis=-1, keepdims=True)
        dp = dot(og, v, ((1,), (1,)))
        ds = (w * (dp - rd) * scale).astype(jnp.bfloat16)
        dq_ref[:, cols] = dot(ds, k, ((1,), (0,))).astype(jnp.bfloat16)
        for parts, acc, left, right in (
            (part_k, acc_k, ds, q),
            (part_v, acc_v, w_low, og),
        ):
            g = dot(left, right, ((0,), (0,)))
            parts[0, :, cols] = g[:rows].astype(jnp.bfloat16)
            acc[:, cols] = g[rows : 2 * rows]
            parts[1, :, cols] = g[2 * rows :].astype(jnp.bfloat16)

    def compute_group(c, carry):
        for side in range(2):

            @pl.when(has[side])
            def _():
                for arr in range(2):
                    kv_copy(1 - side, arr, c, peer[side]).wait_recv()

        for g in range(GROUP):
            one_head(c * width + g * HD)
        for side in range(2):

            @pl.when(has[side])
            def _():
                for arr in range(2):
                    part_copy(side, arr, c, peer[side]).start()

        return carry

    lax.fori_loop(0, groups, compute_group, 0)

    def finish_group(c, carry):
        for side in range(2):

            @pl.when(has[side])
            def _():
                for arr in range(2):
                    part_copy(1 - side, arr, c, peer[side]).wait_recv()

        cols = columns(c)
        for acc, got, out_ref in ((acc_k, got_k, dk_ref), (acc_v, got_v, dv_ref)):
            out_ref[:, cols] = (
                acc[:, cols]
                + got[0, :, cols].astype(jnp.float32)
                + got[1, :, cols].astype(jnp.float32)
            ).astype(out_ref.dtype)
        return carry

    lax.fori_loop(0, groups, finish_group, 0)

    def drain_group(c, carry):
        for side in range(2):

            @pl.when(has[side])
            def _():
                for arr in range(2):
                    kv_copy(side, arr, c, peer[side]).wait_send()
                    part_copy(side, arr, c, peer[side]).wait_send()

        return carry

    lax.fori_loop(0, groups, drain_group, 0)


def shards(count, query_rows, key_rows, value_rows, target_rows, window):
    rows, cols = query_rows.shape
    groups = cols // (GROUP * HD)
    shape = jax.ShapeDtypeStruct((rows, cols), jnp.bfloat16)
    any_spec = pl.BlockSpec(memory_space=pl.ANY)
    vmem_spec = pl.BlockSpec(memory_space=pltpu.VMEM)
    return pl.pallas_call(
        functools.partial(kernel, count),
        out_shape=(shape, shape, shape),
        in_specs=[pl.BlockSpec(memory_space=pltpu.SMEM)] + [any_spec] * 4,
        out_specs=(vmem_spec, vmem_spec, vmem_spec),
        scratch_shapes=[
            pltpu.VMEM((rows, cols), jnp.bfloat16),
            pltpu.VMEM((rows, cols), jnp.bfloat16),
            pltpu.VMEM((3 * rows, cols), jnp.bfloat16),
            pltpu.VMEM((3 * rows, cols), jnp.bfloat16),
            pltpu.VMEM((rows, 3 * rows), jnp.float32),
            pltpu.VMEM((rows, cols), jnp.float32),
            pltpu.VMEM((rows, cols), jnp.float32),
            pltpu.VMEM((2, rows, cols), jnp.bfloat16),
            pltpu.VMEM((2, rows, cols), jnp.bfloat16),
            pltpu.VMEM((2, rows, cols), jnp.bfloat16),
            pltpu.VMEM((2, rows, cols), jnp.bfloat16),
            pltpu.SemaphoreType.DMA((4,)),
            pltpu.SemaphoreType.DMA((2, 2, groups)),
            pltpu.SemaphoreType.DMA((2, 2, groups)),
            pltpu.SemaphoreType.DMA((2, 2, groups)),
            pltpu.SemaphoreType.DMA((2, 2, groups)),
        ],
        compiler_params=pltpu.CompilerParams(
            collective_id=0, has_side_effects=True, vmem_limit_bytes=56 * 1024 * 1024
        ),
    )(window, query_rows, key_rows, value_rows, target_rows)


def solution(mesh):
    spec = P(("clips", "seq"), None)
    return jax.shard_map(
        functools.partial(shards, mesh.shape["seq"]),
        mesh=mesh,
        in_specs=(spec, spec, spec, spec, P()),
        out_specs=(spec, spec, spec),
        check_vma=False,
    )
```

```python
import functools

import jax
import jax.numpy as jnp
from jax import lax
from jax.experimental import pallas as pl
from jax.experimental.pallas import tpu as pltpu
from jax.sharding import PartitionSpec as P

HEADS = 20
HD = 128
BT = 32
GROUP = 4
AHEAD = 3
LOG2E = 1.4426950408889634


def dot(a, b, dims):
    return lax.dot_general(a, b, (dims, ((), ())), preferred_element_type=jnp.float32)


def kernel(
    count,
    planes,
    win_ref,
    q_hbm,
    k_hbm,
    v_hbm,
    t_hbm,
    dq_ref,
    dk_ref,
    dv_ref,
    q_buf,
    t_buf,
    kx,
    vx,
    bias,
    acc_k,
    acc_v,
    part_k,
    part_v,
    got_k,
    got_v,
    relay,
    local_sem,
    sent,
    came,
    relay_send,
    relay_recv,
):
    rows = q_buf.shape[0]
    tiles = rows // BT
    width = GROUP * HD
    groups = q_buf.shape[1] // width
    scale = HD ** (-0.5)
    me = lax.axis_index("seq")
    has = (me > 0, me < count - 1)
    peer = (me - 1, me + 1)
    place = (slice(0, rows), slice(2 * rows, 3 * rows))

    per = 2 * planes
    depth = count // per
    z = me // per
    low = me % per == 0
    high = me % per == per - 1
    up = (GROUP * (depth - 1 - z) + depth // 2) // depth
    down = (GROUP * z + depth // 2) // depth
    relays = planes > 1
    mate = jnp.where(low, me + per - 1, me - per + 1)
    onward = jnp.where(low, me + per, me - per)
    detour = (low & has[0], high & has[1])
    detour_heads = (down, up)
    relay_heads = jnp.where(low, up, down)
    is_relay = (low & (z < depth - 1)) | (high & (z > 0))

    def columns(c):
        return pl.ds(pl.multiple_of(c * width, width), width)

    def head(c, g):
        return pl.ds(pl.multiple_of(c * width + g * HD, HD), HD)

    locals_ = [
        pltpu.make_async_copy(q_hbm, q_buf, local_sem.at[0]),
        pltpu.make_async_copy(k_hbm, kx.at[rows : 2 * rows], local_sem.at[1]),
        pltpu.make_async_copy(v_hbm, vx.at[rows : 2 * rows], local_sem.at[2]),
        pltpu.make_async_copy(t_hbm, t_buf, local_sem.at[3]),
    ]

    def remote(src, dst, send_sem, recv_sem, who):
        return pltpu.make_async_remote_copy(
            src_ref=src,
            dst_ref=dst,
            send_sem=send_sem,
            recv_sem=recv_sem,
            device_id={"seq": who},
            device_id_type=pl.DeviceIdType.MESH,
        )

    def source(side, kind, cols):
        if kind < 2:
            return (k_hbm, v_hbm)[kind].at[:, cols]
        return (part_k, part_v)[kind - 2].at[side, :, cols]

    def landing(side, kind, cols):
        if kind < 2:
            return (kx, vx)[kind].at[place[side], cols]
        return (got_k, got_v)[kind - 2].at[side, :, cols]

    def group_copy(side, kind, c, who):
        cols = columns(c)
        return remote(
            source(side, kind, cols),
            landing(1 - side, kind, cols),
            sent.at[side, kind, c],
            came.at[1 - side, kind, c],
            who,
        )

    def head_copy(side, kind, c, g, who):
        cols = head(c, g)
        return remote(
            source(side, kind, cols),
            landing(1 - side, kind, cols),
            sent.at[side, kind, c],
            came.at[1 - side, kind, c],
            who,
        )

    def mate_copy(side, kind, c, g):
        cols = head(c, g)
        return remote(
            source(side, kind, cols),
            relay.at[kind, :, cols],
            sent.at[side, kind, c],
            relay_recv.at[kind, c * GROUP + g],
            mate,
        )

    def onward_copy(side, kind, c, g):
        cols = head(c, g)
        return remote(
            relay.at[kind, :, cols],
            landing(1 - side, kind, cols),
            relay_send.at[kind, c * GROUP + g],
            came.at[1 - side, kind, c],
            onward,
        )

    def send(kinds, c):
        for side in range(2):
            if not relays:

                @pl.when(has[side])
                def _():
                    for kind in kinds:
                        group_copy(side, kind, c, peer[side]).start()

                continue

            @pl.when(has[side] & jnp.logical_not(detour[side]))
            def _():
                for kind in kinds:
                    group_copy(side, kind, c, peer[side]).start()

            @pl.when(detour[side])
            def _():
                for g in range(GROUP):

                    @pl.when(g < detour_heads[side])
                    def _():
                        for kind in kinds:
                            mate_copy(side, kind, c, g).start()

                    @pl.when(g >= detour_heads[side])
                    def _():
                        for kind in kinds:
                            head_copy(side, kind, c, g, peer[side]).start()

    def await_group(kinds, c):
        for side in range(2):

            @pl.when(has[side])
            def _():
                for kind in kinds:
                    group_copy(1 - side, kind, c, peer[side]).wait_recv()

    def forward(kinds, c, finish=False):
        if not relays:
            return
        for side, end in ((1, low), (0, high)):

            @pl.when(end & is_relay)
            def _():
                for g in range(GROUP):

                    @pl.when(g < relay_heads)
                    def _():
                        for kind in kinds:
                            if finish:
                                onward_copy(side, kind, c, g).wait_send()
                            else:
                                mate_copy(side, kind, c, g).wait_recv()
                                onward_copy(side, kind, c, g).start()

    barrier = pltpu.get_barrier_semaphore()

    def greet(who):
        pl.semaphore_signal(
            barrier, inc=1, device_id={"seq": who}, device_id_type=pl.DeviceIdType.MESH
        )

    greeted = has[0].astype(jnp.int32) + has[1].astype(jnp.int32)
    for side in range(2):

        @pl.when(has[side])
        def _():
            greet(peer[side])

    if relays:
        end = low | high
        before, after = end & (z > 0), end & (z < depth - 1)
        for cond, who in ((end, mate), (before, me - per), (after, me + per)):

            @pl.when(cond)
            def _():
                greet(who)

            greeted = greeted + cond.astype(jnp.int32)
    for copy in locals_:
        copy.start()
    pl.semaphore_wait(barrier, greeted)

    def send_group(c, carry):
        send((0, 1), c)
        return carry

    lax.fori_loop(0, AHEAD, send_group, 0)

    for side in range(2):

        @pl.when(jnp.logical_not(has[side]))
        def _():
            for buf in (kx, vx):
                buf[place[side]] = jnp.zeros((rows, buf.shape[1]), buf.dtype)
            for buf in (got_k, got_v):
                buf[side] = jnp.zeros(buf.shape[1:], buf.dtype)

    first = me * tiles
    listed = lax.broadcasted_iota(jnp.int32, (1, 3 * rows), 1) // BT + (first - tiles)
    for i in range(tiles):
        row_bias = jnp.full((1, 3 * rows), -1e30, jnp.float32)
        for j in range(win_ref.shape[0]):
            entry = win_ref[j, first + i]
            row_bias = jnp.where((listed == entry) & (listed >= 0), 0.0, row_bias)
        bias[i * BT : (i + 1) * BT] = jnp.broadcast_to(row_bias, (BT, 3 * rows))

    for copy in locals_:
        copy.wait()

    def one_head(col):
        cols = pl.ds(pl.multiple_of(col, HD), HD)
        q = q_buf[:, cols]
        k = kx[:, cols]
        v = vx[:, cols]
        s = dot(q, k, ((1,), (1,))) + bias[...]
        top = jnp.max(s, axis=-1, keepdims=True)
        e = jnp.exp2((s - top) * (scale * LOG2E))
        w = e * (1.0 / jnp.sum(e, axis=-1, keepdims=True))
        w_low = w.astype(jnp.bfloat16)
        out = dot(w_low, v, ((1,), (0,)))
        og = (out - t_buf[:, cols].astype(jnp.float32)).astype(jnp.bfloat16)
        rd = jnp.sum(og.astype(jnp.float32) * out, axis=-1, keepdims=True)
        dp = dot(og, v, ((1,), (1,)))
        ds = (w * (dp - rd) * scale).astype(jnp.bfloat16)
        dq_ref[:, cols] = dot(ds, k, ((1,), (0,))).astype(jnp.bfloat16)
        for parts, acc, left, right in (
            (part_k, acc_k, ds, q),
            (part_v, acc_v, w_low, og),
        ):
            g = dot(left, right, ((0,), (0,)))
            parts[0, :, cols] = g[:rows].astype(jnp.bfloat16)
            acc[:, cols] = g[rows : 2 * rows]
            parts[1, :, cols] = g[2 * rows :].astype(jnp.bfloat16)

    def compute_group(c, carry):
        forward((0, 1), c)
        await_group((0, 1), c)
        for g in range(GROUP):
            one_head(c * width + g * HD)
        send((2, 3), c)
        if AHEAD < groups:

            @pl.when(c + AHEAD < groups)
            def _():
                send((0, 1), c + AHEAD)

        @pl.when(c > 0)
        def _():
            forward((2, 3), c - 1)

        return carry

    lax.fori_loop(0, groups, compute_group, 0)
    forward((2, 3), groups - 1)

    def finish_group(c, carry):
        await_group((2, 3), c)
        cols = columns(c)
        for acc, got, out_ref in ((acc_k, got_k, dk_ref), (acc_v, got_v, dv_ref)):
            out_ref[:, cols] = (
                acc[:, cols]
                + got[0, :, cols].astype(jnp.float32)
                + got[1, :, cols].astype(jnp.float32)
            ).astype(out_ref.dtype)
        return carry

    lax.fori_loop(0, groups, finish_group, 0)

    def drain_group(c, carry):
        for side in range(2):

            @pl.when(has[side])
            def _():
                for kind in range(4):
                    group_copy(side, kind, c, peer[side]).wait_send()

        forward((0, 1, 2, 3), c, finish=True)
        return carry

    lax.fori_loop(0, groups, drain_group, 0)


def shards(count, planes, query_rows, key_rows, value_rows, target_rows, window):
    rows, cols = query_rows.shape
    groups = cols // (GROUP * HD)
    shape = jax.ShapeDtypeStruct((rows, cols), jnp.bfloat16)
    any_spec = pl.BlockSpec(memory_space=pl.ANY)
    vmem_spec = pl.BlockSpec(memory_space=pltpu.VMEM)
    return pl.pallas_call(
        functools.partial(kernel, count, planes),
        out_shape=(shape, shape, shape),
        in_specs=[pl.BlockSpec(memory_space=pltpu.SMEM)] + [any_spec] * 4,
        out_specs=(vmem_spec, vmem_spec, vmem_spec),
        scratch_shapes=[
            pltpu.VMEM((rows, cols), jnp.bfloat16),
            pltpu.VMEM((rows, cols), jnp.bfloat16),
            pltpu.VMEM((3 * rows, cols), jnp.bfloat16),
            pltpu.VMEM((3 * rows, cols), jnp.bfloat16),
            pltpu.VMEM((rows, 3 * rows), jnp.float32),
            pltpu.VMEM((rows, cols), jnp.float32),
            pltpu.VMEM((rows, cols), jnp.float32),
            pltpu.VMEM((2, rows, cols), jnp.bfloat16),
            pltpu.VMEM((2, rows, cols), jnp.bfloat16),
            pltpu.VMEM((2, rows, cols), jnp.bfloat16),
            pltpu.VMEM((2, rows, cols), jnp.bfloat16),
            pltpu.VMEM((4, rows, cols), jnp.bfloat16),
            pltpu.SemaphoreType.DMA((4,)),
            pltpu.SemaphoreType.DMA((2, 4, groups)),
            pltpu.SemaphoreType.DMA((2, 4, groups)),
            pltpu.SemaphoreType.DMA((4, HEADS)),
            pltpu.SemaphoreType.DMA((4, HEADS)),
        ],
        compiler_params=pltpu.CompilerParams(
            collective_id=0, has_side_effects=True, vmem_limit_bytes=56 * 1024 * 1024
        ),
    )(window.T, query_rows, key_rows, value_rows, target_rows)


def solution(mesh):
    spec = P(("clips", "seq"), None)
    return jax.shard_map(
        functools.partial(shards, mesh.shape["seq"], 4 // mesh.shape["clips"]),
        mesh=mesh,
        in_specs=(spec, spec, spec, spec, P()),
        out_specs=(spec, spec, spec),
        check_vma=False,
    )
```

```python
import functools

import jax
import jax.numpy as jnp
from jax import lax
from jax.experimental import pallas as pl
from jax.experimental.pallas import tpu as pltpu
from jax.sharding import PartitionSpec as P

HEADS = 20
HD = 128
BT = 32
GROUP = 4
AHEAD = 3
LAG = 2
SHARES = 4
LOG2E = 1.4426950408889634


def dot(a, b, dims):
    return lax.dot_general(a, b, (dims, ((), ())), preferred_element_type=jnp.float32)


def kernel(
    count,
    planes,
    win_ref,
    q_hbm,
    k_hbm,
    v_hbm,
    t_hbm,
    dq_ref,
    dk_ref,
    dv_ref,
    q_buf,
    t_buf,
    kx,
    vx,
    bias,
    acc_k,
    acc_v,
    part_k,
    part_v,
    got_k,
    got_v,
    relay,
    local_sem,
    sent,
    came,
    relay_send,
    relay_recv,
):
    rows = q_buf.shape[0]
    tiles = rows // BT
    width = GROUP * HD
    groups = q_buf.shape[1] // width
    scale = HD ** (-0.5)
    me = lax.axis_index("seq")
    has = (me > 0, me < count - 1)
    peer = (me - 1, me + 1)
    place = (slice(0, rows), slice(2 * rows, 3 * rows))

    per = 2 * planes
    depth = count // per
    z = me // per
    low = me % per == 0
    high = me % per == per - 1
    up = (SHARES * (depth - 1 - z) + depth // 2) // depth
    down = (SHARES * z + depth // 2) // depth
    relays = planes > 1
    mate = jnp.where(low, me + per - 1, me - per + 1)
    onward = jnp.where(low, me + per, me - per)
    detour = (low & has[0], high & has[1])
    detour_heads = (down, up)
    relay_heads = jnp.where(low, up, down)
    is_relay = (low & (z < depth - 1)) | (high & (z > 0))

    def columns(c):
        return pl.ds(pl.multiple_of(c * width, width), width)

    def rank(c, g):
        h = c * GROUP + g
        return h % 2 * 2 + h // 2 % 2

    def head(c, g):
        return pl.ds(pl.multiple_of(c * width + g * HD, HD), HD)

    locals_ = [
        pltpu.make_async_copy(q_hbm, q_buf, local_sem.at[0]),
        pltpu.make_async_copy(k_hbm, kx.at[rows : 2 * rows], local_sem.at[1]),
        pltpu.make_async_copy(v_hbm, vx.at[rows : 2 * rows], local_sem.at[2]),
        pltpu.make_async_copy(t_hbm, t_buf, local_sem.at[3]),
    ]

    def remote(src, dst, send_sem, recv_sem, who):
        return pltpu.make_async_remote_copy(
            src_ref=src,
            dst_ref=dst,
            send_sem=send_sem,
            recv_sem=recv_sem,
            device_id={"seq": who},
            device_id_type=pl.DeviceIdType.MESH,
        )

    def source(side, kind, cols):
        if kind < 2:
            return (k_hbm, v_hbm)[kind].at[:, cols]
        return (part_k, part_v)[kind - 2].at[side, :, cols]

    def landing(side, kind, cols):
        if kind < 2:
            return (kx, vx)[kind].at[place[side], cols]
        return (got_k, got_v)[kind - 2].at[side, :, cols]

    def group_copy(side, kind, c, who):
        cols = columns(c)
        return remote(
            source(side, kind, cols),
            landing(1 - side, kind, cols),
            sent.at[side, kind, c],
            came.at[1 - side, kind, c],
            who,
        )

    def head_copy(side, kind, c, g, who):
        cols = head(c, g)
        return remote(
            source(side, kind, cols),
            landing(1 - side, kind, cols),
            sent.at[side, kind, c],
            came.at[1 - side, kind, c],
            who,
        )

    def mate_copy(side, kind, c, g):
        cols = head(c, g)
        return remote(
            source(side, kind, cols),
            relay.at[kind, :, cols],
            sent.at[side, kind, c],
            relay_recv.at[kind, c * GROUP + g],
            mate,
        )

    def onward_copy(side, kind, c, g):
        cols = head(c, g)
        return remote(
            relay.at[kind, :, cols],
            landing(1 - side, kind, cols),
            relay_send.at[kind, c * GROUP + g],
            came.at[1 - side, kind, c],
            onward,
        )

    def send(kinds, c):
        for side in range(2):
            if not relays:

                @pl.when(has[side])
                def _():
                    for kind in kinds:
                        group_copy(side, kind, c, peer[side]).start()

                continue

            @pl.when(has[side] & jnp.logical_not(detour[side]))
            def _():
                for kind in kinds:
                    group_copy(side, kind, c, peer[side]).start()

            @pl.when(detour[side])
            def _():
                for g in range(GROUP):

                    @pl.when(rank(c, g) < detour_heads[side])
                    def _():
                        for kind in kinds:
                            mate_copy(side, kind, c, g).start()

                    @pl.when(rank(c, g) >= detour_heads[side])
                    def _():
                        for kind in kinds:
                            head_copy(side, kind, c, g, peer[side]).start()

    def await_group(kinds, c):
        for side in range(2):

            @pl.when(has[side])
            def _():
                for kind in kinds:
                    group_copy(1 - side, kind, c, peer[side]).wait_recv()

    def forward(kinds, c, finish=False):
        if not relays:
            return
        for side, end in ((1, low), (0, high)):

            @pl.when(end & is_relay)
            def _():
                for g in range(GROUP):

                    @pl.when(rank(c, g) < relay_heads)
                    def _():
                        for kind in kinds:
                            if finish:
                                onward_copy(side, kind, c, g).wait_send()
                            else:
                                mate_copy(side, kind, c, g).wait_recv()
                                onward_copy(side, kind, c, g).start()

    barrier = pltpu.get_barrier_semaphore()

    def greet(who):
        pl.semaphore_signal(
            barrier, inc=1, device_id={"seq": who}, device_id_type=pl.DeviceIdType.MESH
        )

    greeted = has[0].astype(jnp.int32) + has[1].astype(jnp.int32)
    for side in range(2):

        @pl.when(has[side])
        def _():
            greet(peer[side])

    if relays:
        end = low | high
        before, after = end & (z > 0), end & (z < depth - 1)
        for cond, who in ((end, mate), (before, me - per), (after, me + per)):

            @pl.when(cond)
            def _():
                greet(who)

            greeted = greeted + cond.astype(jnp.int32)
    for copy in locals_:
        copy.start()
    pl.semaphore_wait(barrier, greeted)

    def send_group(c, carry):
        send((0, 1), c)
        return carry

    lax.fori_loop(0, AHEAD, send_group, 0)

    for side in range(2):

        @pl.when(jnp.logical_not(has[side]))
        def _():
            for buf in (kx, vx):
                buf[place[side]] = jnp.zeros((rows, buf.shape[1]), buf.dtype)
            for buf in (got_k, got_v):
                buf[side] = jnp.zeros(buf.shape[1:], buf.dtype)

    first = me * tiles
    listed = lax.broadcasted_iota(jnp.int32, (1, 3 * rows), 1) // BT + (first - tiles)
    for i in range(tiles):
        row_bias = jnp.full((1, 3 * rows), -1e30, jnp.float32)
        for j in range(win_ref.shape[0]):
            entry = win_ref[j, first + i]
            row_bias = jnp.where((listed == entry) & (listed >= 0), 0.0, row_bias)
        bias[i * BT : (i + 1) * BT] = jnp.broadcast_to(row_bias, (BT, 3 * rows))

    for copy in locals_:
        copy.wait()

    def one_head(col):
        cols = pl.ds(pl.multiple_of(col, HD), HD)
        q = q_buf[:, cols]
        k = kx[:, cols]
        v = vx[:, cols]
        s = dot(q, k, ((1,), (1,))) + bias[...]
        top = jnp.max(s, axis=-1, keepdims=True)
        e = jnp.exp2((s - top) * (scale * LOG2E))
        w = e * (1.0 / jnp.sum(e, axis=-1, keepdims=True))
        w_low = w.astype(jnp.bfloat16)
        out = dot(w_low, v, ((1,), (0,)))
        og = (out - t_buf[:, cols].astype(jnp.float32)).astype(jnp.bfloat16)
        rd = jnp.sum(og.astype(jnp.float32) * out, axis=-1, keepdims=True)
        dp = dot(og, v, ((1,), (1,)))
        ds = (w * (dp - rd) * scale).astype(jnp.bfloat16)
        dq_ref[:, cols] = dot(ds, k, ((1,), (0,))).astype(jnp.bfloat16)
        for parts, acc, left, right in (
            (part_k, acc_k, ds, q),
            (part_v, acc_v, w_low, og),
        ):
            g = dot(left, right, ((0,), (0,)))
            parts[0, :, cols] = g[:rows].astype(jnp.bfloat16)
            acc[:, cols] = g[rows : 2 * rows]
            parts[1, :, cols] = g[2 * rows :].astype(jnp.bfloat16)

    def compute_group(c, carry):
        @pl.when(c >= LAG)
        def _():
            forward((2, 3), c - LAG)

        forward((0, 1), c)
        await_group((0, 1), c)
        for g in range(GROUP):
            one_head(c * width + g * HD)
        send((2, 3), c)
        if AHEAD < groups:

            @pl.when(c + AHEAD < groups)
            def _():
                send((0, 1), c + AHEAD)

        return carry

    lax.fori_loop(0, groups, compute_group, 0)

    def forward_group(c, carry):
        forward((2, 3), c)
        return carry

    lax.fori_loop(max(groups - LAG, 0), groups, forward_group, 0)

    def finish_group(c, carry):
        await_group((2, 3), c)
        cols = columns(c)
        for acc, got, out_ref in ((acc_k, got_k, dk_ref), (acc_v, got_v, dv_ref)):
            out_ref[:, cols] = (
                acc[:, cols]
                + got[0, :, cols].astype(jnp.float32)
                + got[1, :, cols].astype(jnp.float32)
            ).astype(out_ref.dtype)
        return carry

    lax.fori_loop(0, groups, finish_group, 0)

    def drain_group(c, carry):
        for side in range(2):

            @pl.when(has[side])
            def _():
                for kind in range(4):
                    group_copy(side, kind, c, peer[side]).wait_send()

        forward((0, 1, 2, 3), c, finish=True)
        return carry

    lax.fori_loop(0, groups, drain_group, 0)


def write_out(*refs):
    copies = [pltpu.make_async_copy(refs[i], refs[i + 3], refs[6].at[i]) for i in range(3)]
    for copy in copies:
        copy.start()
    for copy in copies:
        copy.wait()


def shards(count, planes, query_rows, key_rows, value_rows, target_rows, window):
    rows, cols = query_rows.shape
    groups = cols // (GROUP * HD)
    shape = jax.ShapeDtypeStruct((rows, cols), jnp.bfloat16)
    any_spec = pl.BlockSpec(memory_space=pltpu.HBM)
    vmem_spec = pl.BlockSpec(memory_space=pltpu.VMEM)
    near = pltpu.VMEM((rows, cols), jnp.bfloat16)
    grads = pl.pallas_call(
        functools.partial(kernel, count, planes),
        out_shape=(near, near, near),
        in_specs=[pl.BlockSpec(memory_space=pltpu.SMEM)] + [any_spec] * 4,
        out_specs=(vmem_spec, vmem_spec, vmem_spec),
        scratch_shapes=[
            pltpu.VMEM((rows, cols), jnp.bfloat16),
            pltpu.VMEM((rows, cols), jnp.bfloat16),
            pltpu.VMEM((3 * rows, cols), jnp.bfloat16),
            pltpu.VMEM((3 * rows, cols), jnp.bfloat16),
            pltpu.VMEM((rows, 3 * rows), jnp.float32),
            pltpu.VMEM((rows, cols), jnp.float32),
            pltpu.VMEM((rows, cols), jnp.float32),
            pltpu.VMEM((2, rows, cols), jnp.bfloat16),
            pltpu.VMEM((2, rows, cols), jnp.bfloat16),
            pltpu.VMEM((2, rows, cols), jnp.bfloat16),
            pltpu.VMEM((2, rows, cols), jnp.bfloat16),
            pltpu.VMEM((4, rows, cols), jnp.bfloat16),
            pltpu.SemaphoreType.DMA((4,)),
            pltpu.SemaphoreType.DMA((2, 4, groups)),
            pltpu.SemaphoreType.DMA((2, 4, groups)),
            pltpu.SemaphoreType.DMA((4, HEADS)),
            pltpu.SemaphoreType.DMA((4, HEADS)),
        ],
        compiler_params=pltpu.CompilerParams(
            collective_id=0, has_side_effects=True, vmem_limit_bytes=57 * 1024 * 1024
        ),
    )(window.T, query_rows, key_rows, value_rows, target_rows)
    grads = [pltpu.with_memory_space_constraint(grad, pltpu.VMEM) for grad in grads]
    return pl.pallas_call(
        write_out,
        out_shape=(shape, shape, shape),
        in_specs=[vmem_spec] * 3,
        out_specs=(any_spec, any_spec, any_spec),
        scratch_shapes=[pltpu.SemaphoreType.DMA((3,))],
    )(*grads)


def solution(mesh):
    spec = P(("clips", "seq"), None)
    return jax.shard_map(
        functools.partial(shards, mesh.shape["seq"], 4 // mesh.shape["clips"]),
        mesh=mesh,
        in_specs=(spec, spec, spec, spec, P()),
        out_specs=(spec, spec, spec),
        check_vma=False,
    )
```
